32 devices in a mesh: req: 2 (over x), hst: 16 (over z, y, core).
Axes of the slice: x: 2, y: 2, z: 4, core: 2. Of those that a mesh axis runs over, the one named last changes fastest.
Arguments:
- ctx_q: bfloat16 [4096, 4096], P(('req', 'hst')), parts along dimension 0, may hold values from -24 to 24
- ctx_k: bfloat16 [4096, 512], P(('req', 'hst')), parts along dimension 0, may hold values from -8 to 8
- ctx_v: bfloat16 [4096, 512], P(('req', 'hst')), parts along dimension 0, may hold values from -6 to 6
- ask_q: bfloat16 [64, 4096], P(('req', 'hst')), parts along dimension 0, may hold values from -24 to 24
- ask_k: bfloat16 [64, 512], P(('req', 'hst')), parts along dimension 0, may hold values from -9 to 9
- ask_v: bfloat16 [64, 512], P(('req', 'hst')), parts along dimension 0, may hold values from -6 to 6
- valid: int32 [32], P(('req', 'hst')), parts along dimension 0, may hold values from 64 to 128, as said below
Outputs:
- ctx_out: bfloat16 [4096, 4096], P(('req', 'hst')), parts along dimension 0
- ask_out: bfloat16 [64, 4096], P(('req', 'hst')), parts along dimension 0
The draws below stay inside these ranges and needn't reach their ends.
There are 2 independent parts, one for each index of `req`. The reference program is written for one: setup_inputs(seed, part) draws one part's arguments, and reference() takes and returns one part's arrays. A program takes and returns all parts, laid end to end along the dimension named above; each array names one. Nothing has to cross between parts.
Inputs may be any that keep to these rules, and one draw needn't show every extreme that they name: `valid`: block 0, the anchor, is always full.
All inputs are finite; a program needn't handle non-finite values.
Results may differ from the reference program's by a relative error of at most 0.0029.
Values may be sent and summed in bfloat16 or wider, within the bound.
A program may use at most 320 MiB of HBM per device.

```python
import math
import jax
import jax.numpy as jnp
from jax import lax

H = 32
KVH = 4
DH = 128
BLOCK = 128
TOKENS = 2048
QLEN = 32
N_HST = 16


def draw_ctx_q(key, part):
    values = jnp.clip(jax.random.normal(jax.random.fold_in(key, 1), (TOKENS, H * DH)) * 2.5, -10.0, 10.0)
    return values.astype(jnp.bfloat16)


def draw_ctx_k(key, part):
    values = jnp.clip(jax.random.normal(jax.random.fold_in(key, 5), (TOKENS, KVH * DH)), -6.0, 6.0)
    return values.astype(jnp.bfloat16)


def draw_ask_q(key, part):
    values = jnp.clip(jax.random.normal(jax.random.fold_in(key, 11), (QLEN, H * DH)) * 2.5, -10.0, 10.0)
    return values.astype(jnp.bfloat16)


def draw_valid(key, part):
    host_count = TOKENS // BLOCK
    counts = jax.random.randint(jax.random.fold_in(key, 21), (host_count,), BLOCK // 2, BLOCK + 1)
    lowest = jax.random.randint(jax.random.fold_in(key, 22), (), 1, host_count)
    counts = counts.at[lowest].set(BLOCK // 2)
    counts = counts.at[0].set(BLOCK)
    return counts.astype(jnp.int32)


def block_scale(key, dims, cuts, smallest, high):
    loudness = 1.0
    for axis_at, parts in cuts:
        steps = jax.random.uniform(jax.random.fold_in(jax.random.fold_in(key, 6), axis_at), (parts,), jnp.float32, smallest / len(cuts), high / len(cuts))
        loudness = loudness * jnp.repeat(jnp.exp(steps), dims[axis_at] // parts).reshape((-1,) + (1,) * (len(dims) - 1 - axis_at))
    return loudness


def normal_values(stream_key, shape, spread, limit, cuts=(), held_as=jnp.bfloat16):
    loudness = block_scale(stream_key, shape, cuts, -0.22, 0.18) if cuts else 1.0
    result = jax.random.normal(stream_key, shape, jnp.float32) * spread * loudness
    return jnp.minimum(jnp.maximum(result, -limit), limit).astype(held_as)


def setup_inputs(seed: int = 0, part: int = 0) -> dict:
    seeds = jax.random.split(jax.random.key(seed), 8)
    part_splits = jax.random.split(jax.random.fold_in(seeds[7], part), 8)
    ctx_q = draw_ctx_q(jax.random.fold_in(jax.random.fold_in(seeds[7], part), 71), part)
    ctx_k = draw_ctx_k(jax.random.fold_in(jax.random.fold_in(seeds[7], part), 71), part)
    ctx_v = normal_values(part_splits[2], (TOKENS, KVH * DH), 1.0, 6.0, ((0, 16),))
    ask_q = draw_ask_q(jax.random.fold_in(jax.random.fold_in(seeds[7], part), 71), part)
    ask_k = normal_values(part_splits[4], (QLEN, KVH * DH), 1.5, 9.0, ((0, 16),))
    ask_v = normal_values(part_splits[5], (QLEN, KVH * DH), 1.0, 6.0, ((0, 16),))
    valid = draw_valid(jax.random.fold_in(jax.random.fold_in(seeds[7], part), 71), part)
    return dict(ctx_q=ctx_q, ctx_k=ctx_k, ctx_v=ctx_v, ask_q=ask_q, ask_k=ask_k, ask_v=ask_v, valid=valid)


def partial_attend(queries, key_rows, value_rows, visible):
    row_count = queries.shape[0]
    span_count = key_rows.shape[0]
    group_size = H // KVH
    query_f = queries.astype(jnp.float32).reshape(row_count, KVH, group_size, DH)
    key_f = key_rows.astype(jnp.float32).reshape(span_count, KVH, DH)
    value_f = value_rows.astype(jnp.float32).reshape(span_count, KVH, DH)
    scores = jnp.einsum('rkgd,skd->rkgs', query_f, key_f) * (1.0 / math.sqrt(DH))
    scores = jnp.where(visible[:, None, None, :], scores, -jnp.inf)
    row_max = lax.optimization_barrier(jnp.max(scores, axis=-1))
    expon = jnp.exp(scores - row_max[..., None])
    row_sum = lax.optimization_barrier(jnp.sum(expon, axis=-1))
    rounded = lax.optimization_barrier(expon.astype(jnp.bfloat16)).astype(jnp.float32)
    mixed = jnp.einsum('rkgs,skd->rkgd', rounded, value_f)
    return (row_max.reshape(row_count, H), row_sum.reshape(row_count, H), mixed.reshape(row_count, H * DH))

def weigh(values, factor):
    shape = values.shape
    return (values.reshape(shape[:-1] + (H, DH)) * factor[..., None]).reshape(shape)

def reference(ctx_q, ctx_k, ctx_v, ask_q, ask_k, ask_v, valid):
    local = jnp.arange(BLOCK, dtype=jnp.int32)
    anchor_k = ctx_k[:BLOCK]
    anchor_v = ctx_v[:BLOCK]

    def context_block(block_index):
        start = (block_index * BLOCK).astype(jnp.int32)
        queries = lax.dynamic_slice_in_dim(ctx_q, start, BLOCK, 0)
        own_k = lax.dynamic_slice_in_dim(ctx_k, start, BLOCK, 0)
        own_v = lax.dynamic_slice_in_dim(ctx_v, start, BLOCK, 0)
        valid_count = valid[block_index]
        own_visible = (local[None, :] <= local[:, None]) & (local[None, :] < valid_count)
        anchor_visible = jnp.broadcast_to(block_index > 0, (BLOCK, BLOCK))
        visible = jnp.concatenate([anchor_visible, own_visible], axis=1)
        row_max, row_sum, mixed = partial_attend(queries, jnp.concatenate([anchor_k, own_k], 0), jnp.concatenate([anchor_v, own_v], 0), visible)
        normed = weigh(mixed, 1.0 / row_sum)
        return jnp.where(local[:, None] < valid_count, normed, 0.0).astype(jnp.bfloat16)
    ctx_out = lax.map(context_block, jnp.arange(N_HST, dtype=jnp.int32)).reshape(TOKENS, H * DH)
    query_pos = jnp.arange(QLEN, dtype=jnp.int32)
    causal = query_pos[None, :] <= query_pos[:, None]

    def host_step(carry, block_index):
        best, total, summed = carry
        start = (block_index * BLOCK).astype(jnp.int32)
        own_k = lax.dynamic_slice_in_dim(ctx_k, start, BLOCK, 0)
        own_v = lax.dynamic_slice_in_dim(ctx_v, start, BLOCK, 0)
        valid_count = valid[block_index]
        visible = jnp.concatenate([jnp.broadcast_to(local[None, :] < valid_count, (QLEN, BLOCK)), causal & (block_index == N_HST - 1)], axis=1)
        row_max, row_sum, mixed = partial_attend(ask_q, jnp.concatenate([own_k, ask_k], 0), jnp.concatenate([own_v, ask_v], 0), visible)
        new_best = jnp.maximum(best, row_max)
        old_weight = jnp.exp(best - new_best)
        new_weight = jnp.exp(row_max - new_best)
        return ((new_best, total * old_weight + row_sum * new_weight, weigh(summed, old_weight) + weigh(mixed, new_weight)), None)
    start_carry = (jnp.full((QLEN, H), -jnp.inf, jnp.float32), jnp.zeros((QLEN, H), jnp.float32), jnp.zeros((QLEN, H * DH), jnp.float32))
    (best, total, summed), _ = lax.scan(host_step, start_carry, jnp.arange(N_HST, dtype=jnp.int32))
    ask_out = weigh(summed, 1.0 / total).astype(jnp.bfloat16)
    return (ctx_out, ask_out)
```

```python
import functools
import math

import jax
import jax.numpy as jnp
from jax import lax
from jax.experimental import pallas as pl
from jax.experimental.pallas import tpu as pltpu
from jax.sharding import PartitionSpec as P

H = 32
KVH = 4
DH = 128
G = H // KVH
C = math.log2(math.e) / math.sqrt(DH)
NT = (((1,), (1,)), ((), ()))
NN = (((1,), (0,)), ((), ()))


def remote(src, dst, send_sem, recv_sem, target):
    return pltpu.make_async_remote_copy(
        src_ref=src,
        dst_ref=dst,
        send_sem=send_sem,
        recv_sem=recv_sem,
        device_id={"hst": target},
        device_id_type=pl.DeviceIdType.MESH,
    )


def kernel(
    n, ctx_q, ctx_k, ctx_v, pack, ctx_out, ask_out,
    qbuf, obuf, kc, kvall, cnt, qall, selfkv, num, numr, fin,
    s_kv, s_an, s_q, s_out, s_own,
    q_s, q_r, k_s, k_r, c_s, c_r, a_s, a_r, f_s, r_s, n_s, n_r, o_s, o_r,
):
    rows = ctx_q.shape[0]
    tile = pack.shape[2]
    tokens = tile // G
    planes = n // KVH
    span = KVH * tile
    me = lax.axis_index("hst")
    p = me // KVH
    m = me % KVH
    is_root = me == 0
    is_last = p == planes - 1
    low = m // 2 * 2
    far = (m + 2) % KVH

    def cols(g):
        return pl.ds(pl.multiple_of(g * DH, DH), DH)

    def wide(g):
        return pl.ds(pl.multiple_of(g * (G * DH), G * DH), G * DH)

    def load_kv(g, i, half, sem):
        src = (ctx_k, ctx_v)[i]
        return pltpu.make_async_copy(src.at[:, cols(g)], kc.at[g, i, half], sem.at[g, i])

    for g in range(KVH):
        for i in range(2):
            load_kv(g, i, 1, s_kv).start()

    @pl.when(is_root)
    def _():
        for g in range(KVH):
            for i in range(2):
                load_kv(g, i, 0, s_an).start()

    own_copies = [
        pltpu.make_async_copy(pack.at[m, 0], qall.at[me], s_own.at[0]),
        pltpu.make_async_copy(pack.at[0, 3], cnt.at[m], s_own.at[1]),
        pltpu.make_async_copy(ctx_k.at[:, cols(m)], kvall.at[m, 0], s_own.at[2]),
        pltpu.make_async_copy(ctx_v.at[:, cols(m)], kvall.at[m, 1], s_own.at[3]),
    ]
    own_self = pltpu.make_async_copy(pack.at[m, pl.ds(1, 2)], selfkv.at[me], s_own.at[4])
    q_loads = [
        pltpu.make_async_copy(ctx_q.at[:, wide(g)], qbuf.at[:, wide(g)], s_q.at[g])
        for g in range(KVH)
    ]
    for copy in own_copies:
        copy.start()

    @pl.when(is_last)
    def _():
        own_self.start()

    for copy in q_loads:
        copy.start()

    barrier = pltpu.get_barrier_semaphore()

    @pl.loop(1, n)
    def _(d):
        pl.semaphore_signal(
            barrier, inc=1, device_id={"hst": (me + d) % n}, device_id_type=pl.DeviceIdType.MESH
        )

    pl.semaphore_wait(barrier, n - 1)

    def q_send(d):
        target = (me + d) % n
        return remote(pack.at[target % KVH, 0], qall.at[me], q_s.at[d], q_r.at[me], target)

    @pl.loop(1, n)
    def _(d):
        q_send(d).start()

    def self_send(g):
        return remote(
            pack.at[g, pl.ds(1, 2)], selfkv.at[me], f_s.at[g], r_s.at[me], n - KVH + g
        )

    for g in range(KVH):
        @pl.when(me != n - KVH + g)
        def _():
            self_send(g).start()

    def cnt_send(d):
        g = (m + d) % KVH
        return remote(pack.at[0, 3], cnt.at[m], c_s.at[d], c_r.at[m], p * KVH + g)

    for d in range(1, KVH):
        cnt_send(d).start()

    for g in range(KVH):
        for i in range(2):
            load_kv(g, i, 1, s_kv).wait()

    def chunk_send(g, slot, target):
        piece = kc.at[g, :, 0]
        return remote(piece, piece, a_s.at[g, slot], a_r.at[g], target)

    def across(g):
        return chunk_send(g, 0, p * KVH + far)

    def beside(g):
        return chunk_send(g, 1, p * KVH + m + 1)

    def along(g, q):
        return chunk_send(g, 1 + q, q * KVH + m)

    even = m % 2 == 0
    first = [low, low + 1]
    second = [far // 2 * 2, far // 2 * 2 + 1]

    @pl.when(is_root)
    def _():
        for g in range(KVH):
            for i in range(2):
                load_kv(g, i, 0, s_an).wait()
        for g in (2, 3):
            across(g).start()
        for q in range(planes - 1, 0, -1):
            for g in (0, 1):
                along(g, q).start()

    def kv_send(d):
        g = (m + d) % KVH
        return remote(kc.at[g, :, 1], kvall.at[m], k_s.at[d], k_r.at[m], p * KVH + g)

    for d in (2, 3, 1):
        kv_send(d).start()

    @pl.when(is_root)
    def _():
        for g in (0, 1):
            across(g).start()
        for g in (0, 1, 2, 3):
            beside(g).start()

    def chunk_wait(g):
        chunk_send(g, 0, me).wait_recv()

    hub = (p == 0) & (m == 2)

    def take_first():
        @pl.when(jnp.logical_not(is_root))
        def _():
            for g in first:
                chunk_wait(g)

                @pl.when(hub)
                def _():
                    for q in range(planes - 1, 0, -1):
                        along(g, q).start()

                @pl.when(even & (p > 0))
                def _():
                    across(g).start()

                @pl.when(even)
                def _():
                    beside(g).start()

    def take_second():
        @pl.when(jnp.logical_not(is_root))
        def _():
            for g in second:
                chunk_wait(g)

                @pl.when(even)
                def _():
                    beside(g).start()

    early = hub | ((m == 0) & (p > 0))

    @pl.when(early)
    def _():
        take_first()

    @pl.loop(1, n)
    def _(d):
        source = (me + d) % n
        remote(pack.at[0, 0], qall.at[source], q_s.at[0], q_r.at[source], me).wait_recv()

    for copy in own_copies:
        copy.wait()

    for d in range(1, KVH):
        j = (m + d) % KVH
        remote(pack.at[0, 3], cnt.at[j], c_s.at[0], c_r.at[j], me).wait_recv()
        remote(kc.at[0, :, 1], kvall.at[j], k_s.at[0], k_r.at[j], me).wait_recv()

    def diagonal():
        return lax.broadcasted_iota(jnp.int32, (span, DH), 0) == lax.broadcasted_iota(
            jnp.int32, (span, DH), 1
        )

    def num_send(q):
        return remote(num.at[q], numr.at[p], n_s.at[q], n_r.at[p], q * KVH + m)

    def ask(with_self):
        lane = lax.broadcasted_iota(jnp.int32, (span, rows), 1).astype(jnp.float32)

        @pl.loop(0, planes)
        def _(step):
            q = (p + 1 + step) % planes
            queries = qall[pl.ds(q * KVH, KVH)].reshape(span, DH)
            best = total = summed = None
            for j in range(KVH):
                s = lax.dot_general(queries, kvall[j, 0], NT, preferred_element_type=jnp.float32)
                count = cnt[j].astype(jnp.float32)[0:1, :]
                s = jnp.where(lane < count, s, -jnp.inf)
                top = jnp.max(s, axis=1, keepdims=True)
                if with_self and j == KVH - 1:
                    keys = selfkv[:, 0].reshape(n * tile, DH)
                    values = selfkv[:, 1].reshape(n * tile, DH)
                    s2 = lax.dot_general(queries, keys, NT, preferred_element_type=jnp.float32)
                    shape = (span, n * tile)
                    at = lax.broadcasted_iota(jnp.int32, shape, 1)
                    row = lax.broadcasted_iota(jnp.int32, shape, 0)
                    shift = tile.bit_length() - 1
                    u = (at >> shift) * tokens + (at & (tile - 1))
                    t = (q * KVH + (row >> shift)) * tokens + (
                        (row & (tile - 1)) >> (G.bit_length() - 1)
                    )
                    s2 = jnp.where(((at & (tile - 1)) < tokens) & (u <= t), s2, -jnp.inf)
                    top = jnp.maximum(top, jnp.max(s2, axis=1, keepdims=True))
                e = jnp.exp2((s - top) * C)
                part = jnp.sum(e, axis=1, keepdims=True)
                mixed = lax.dot_general(
                    e.astype(jnp.bfloat16), kvall[j, 1], NN, preferred_element_type=jnp.float32
                )
                if with_self and j == KVH - 1:
                    e2 = jnp.exp2((s2 - top) * C)
                    part = part + jnp.sum(e2, axis=1, keepdims=True)
                    mixed = mixed + lax.dot_general(
                        e2.astype(jnp.bfloat16), values, NN, preferred_element_type=jnp.float32
                    )
                if best is None:
                    best, total, summed = top, part, mixed
                else:
                    peak = jnp.maximum(best, top)
                    old = jnp.exp2((best - peak) * C)
                    new = jnp.exp2((top - peak) * C)
                    best, total, summed = peak, total * old + part * new, summed * old + mixed * new
            num[q, pl.ds(0, span)] = summed
            diag = diagonal()
            line1 = jnp.sum(jnp.where(diag, best, 0.0), axis=0, keepdims=True)
            line2 = jnp.sum(jnp.where(diag, total, 0.0), axis=0, keepdims=True)
            pick = lax.broadcasted_iota(jnp.int32, (8, DH), 0) == 0
            num[q, pl.ds(span, 8)] = jnp.where(pick, line1, line2)

            @pl.when(q != p)
            def _():
                num_send(q).start()

    @pl.when(is_last)
    def _():
        own_self.wait()

        @pl.loop(1, n)
        def _(d):
            source = (me + d) % n
            remote(
                pack.at[0, pl.ds(1, 2)], selfkv.at[source], f_s.at[0], r_s.at[source], me
            ).wait_recv()

        ask(True)

    @pl.when(jnp.logical_not(is_last))
    def _():
        ask(False)

    def out_copy(g):
        return pltpu.make_async_copy(obuf.at[:, wide(g)], ctx_out.at[:, wide(g)], s_out.at[g])

    def context(g):
        pltpu.make_async_copy(ctx_q.at[:, wide(g)], qbuf.at[:, wide(g)], s_q.at[g]).wait()
        count = cnt[m].astype(jnp.float32)[0:1, :]
        row = lax.broadcasted_iota(jnp.int32, (rows, rows), 0)
        lane = lax.broadcasted_iota(jnp.int32, (rows, rows), 1)
        own = (lane <= row) & (lane.astype(jnp.float32) < count)
        outer = jnp.broadcast_to(me, (rows, rows)) > 0
        visible = jnp.concatenate([outer, own], axis=1)
        kept = lax.broadcasted_iota(jnp.int32, (rows, DH), 0).astype(jnp.float32) < count

        @pl.loop(0, G // 2)
        def _(pair):
            for k in range(2):
                at = pl.ds(pl.multiple_of((g * G + pair * 2 + k) * DH, DH), DH)
                keys = kc[g, 0].reshape(2 * rows, DH)
                values = kc[g, 1].reshape(2 * rows, DH)
                s = lax.dot_general(qbuf[:, at], keys, NT, preferred_element_type=jnp.float32)
                s = jnp.where(visible, s, -jnp.inf)
                top = jnp.max(s, axis=1, keepdims=True)
                e = jnp.exp2((s - top) * C)
                total = jnp.sum(e, axis=1, keepdims=True)
                mixed = lax.dot_general(
                    e.astype(jnp.bfloat16), values, NN, preferred_element_type=jnp.float32
                )
                out = jnp.where(kept, mixed * (1.0 / total), 0.0)
                obuf[:, at] = out.astype(jnp.bfloat16)

        out_copy(g).start()

    @pl.when(jnp.logical_not(early))
    def _():
        take_first()

    context(first[0])
    take_second()
    context(first[1])
    context(second[0])

    @pl.loop(1, planes)
    def _(d):
        q = (p + d) % planes
        remote(num.at[0], numr.at[q], n_s.at[0], n_r.at[q], me).wait_recv()

    def columns(block):
        diag = diagonal()
        best = jnp.sum(jnp.where(diag, block[0:1, :], 0.0), axis=1, keepdims=True)
        total = jnp.sum(jnp.where(diag, block[1:2, :], 0.0), axis=1, keepdims=True)
        return best, total

    best, total = columns(num[p, pl.ds(span, 8)])
    summed = num[p, pl.ds(0, span)]
    for d in range(1, planes):
        q = (p + d) % planes
        top, part = columns(numr[q, pl.ds(span, 8)])
        mixed = numr[q, pl.ds(0, span)]
        peak = jnp.maximum(best, top)
        old = jnp.exp2((best - peak) * C)
        new = jnp.exp2((top - peak) * C)
        best, total, summed = peak, total * old + part * new, summed * old + mixed * new
    fin[...] = (summed * (1.0 / total)).astype(jnp.bfloat16).reshape(KVH, tile, DH)

    def fin_send(d):
        j = (m + d) % KVH
        return remote(fin.at[j], ask_out.at[m], o_s.at[d], o_r.at[m], p * KVH + j)

    own_fin = pltpu.make_async_copy(fin.at[m], ask_out.at[m], s_own.at[5])
    for d in range(1, KVH):
        fin_send(d).start()
    own_fin.start()

    context(second[1])

    own_fin.wait()
    for d in range(1, KVH):
        j = (m + d) % KVH
        remote(fin.at[0], ask_out.at[j], o_s.at[0], o_r.at[j], me).wait_recv()
        fin_send(d).wait_send()
        cnt_send(d).wait_send()
        kv_send(d).wait_send()
    for g in range(KVH):
        out_copy(g).wait()

        @pl.when(me != n - KVH + g)
        def _():
            self_send(g).wait_send()

    @pl.loop(1, n)
    def _(d):
        q_send(d).wait_send()

    @pl.loop(1, planes)
    def _(d):
        num_send((p + d) % planes).wait_send()

    @pl.when(is_root)
    def _():
        for g in range(KVH):
            across(g).wait_send()
            beside(g).wait_send()
        for q in range(1, planes):
            for g in (0, 1):
                along(g, q).wait_send()

    @pl.when(even & jnp.logical_not(is_root))
    def _():
        for g in first + second:
            beside(g).wait_send()

        @pl.when(p > 0)
        def _():
            for g in first:
                across(g).wait_send()

    @pl.when(hub)
    def _():
        for g in first:
            for q in range(1, planes):
                along(g, q).wait_send()


def body(n, ctx_q, ctx_k, ctx_v, ask_q, ask_k, ask_v, valid):
    rows = ctx_q.shape[0]
    tokens = ask_q.shape[0]
    tile = tokens * G
    planes = n // KVH
    span = KVH * tile

    def heads(x):
        x = x.reshape(tokens, KVH, -1, DH).transpose(1, 0, 2, 3).reshape(KVH, -1, DH)
        return jnp.pad(x, ((0, 0), (0, tile - x.shape[1]), (0, 0)))

    count = jnp.broadcast_to(valid.astype(jnp.bfloat16).reshape(1, 1, 1), (KVH, tile, DH))
    pack = jnp.stack([heads(ask_q), heads(ask_k), heads(ask_v), count], axis=1)
    dma = pltpu.SemaphoreType.DMA
    bf = jnp.bfloat16
    ctx_out, ask_out = pl.pallas_call(
        functools.partial(kernel, n),
        out_shape=(
            jax.ShapeDtypeStruct(ctx_q.shape, bf),
            jax.ShapeDtypeStruct((KVH, tile, DH), bf),
        ),
        in_specs=[pl.BlockSpec(memory_space=pl.ANY)] * 4,
        out_specs=(pl.BlockSpec(memory_space=pl.ANY),) * 2,
        scratch_shapes=[
            pltpu.VMEM(ctx_q.shape, bf),
            pltpu.VMEM(ctx_q.shape, bf),
            pltpu.VMEM((KVH, 2, 2, rows, DH), bf),
            pltpu.VMEM((KVH, 2, rows, DH), bf),
            pltpu.VMEM((KVH, tile, DH), bf),
            pltpu.VMEM((n, tile, DH), bf),
            pltpu.VMEM((n, 2, tile, DH), bf),
            pltpu.VMEM((planes, span + 8, DH), jnp.float32),
            pltpu.VMEM((planes, span + 8, DH), jnp.float32),
            pltpu.VMEM((KVH, tile, DH), bf),
            dma((KVH, 2)),
            dma((KVH, 2)),
            dma((KVH,)),
            dma((KVH,)),
            dma((6,)),
            dma((n,)),
            dma((n,)),
            dma((KVH,)),
            dma((KVH,)),
            dma((KVH,)),
            dma((KVH,)),
            dma((KVH, planes + 1)),
            dma((KVH,)),
            dma((KVH,)),
            dma((n,)),
            dma((planes,)),
            dma((planes,)),
            dma((KVH,)),
            dma((KVH,)),
        ],
        compiler_params=pltpu.CompilerParams(collective_id=0, has_side_effects=True),
    )(ctx_q, ctx_k, ctx_v, pack)
    ask_out = ask_out.reshape(KVH, tokens, G, DH).transpose(1, 0, 2, 3).reshape(tokens, H * DH)
    return ctx_out, ask_out


def solution(mesh):
    n = mesh.shape["hst"]
    rows = P(("req", "hst"), None)
    return jax.shard_map(
        functools.partial(body, n),
        mesh=mesh,
        in_specs=(rows,) * 6 + (P(("req", "hst")),),
        out_specs=(rows, rows),
        check_vma=False,
    )
```

```python
import functools
import math

import jax
import jax.numpy as jnp
from jax import lax
from jax.experimental import pallas as pl
from jax.experimental.pallas import tpu as pltpu
from jax.sharding import PartitionSpec as P

H = 32
KVH = 4
DH = 128
G = H // KVH
UNROLL = 8
PAIR = 2
C = math.log2(math.e) / math.sqrt(DH)
NT = (((1,), (1,)), ((), ()))
NN = (((1,), (0,)), ((), ()))


def remote(src, dst, send_sem, recv_sem, target):
    return pltpu.make_async_remote_copy(
        src_ref=src,
        dst_ref=dst,
        send_sem=send_sem,
        recv_sem=recv_sem,
        device_id={"hst": target},
        device_id_type=pl.DeviceIdType.MESH,
    )


def kernel(
    n, ctx_q, ctx_k, ctx_v, pack, ctx_out, ask_out,
    qbuf, obuf, kc, kvall, cnt, qall, selfkv, num, numr, fin,
    s_kv, s_an, s_q, s_out, s_own,
    q_s, q_r, k_s, k_r, c_s, c_r, a_s, a_r, f_s, r_s, n_s, n_r, o_s, o_r,
):
    rows = ctx_q.shape[0]
    tile = pack.shape[2]
    tokens = tile // G
    planes = n // KVH
    span = KVH * tile
    me = lax.axis_index("hst")
    p = me // KVH
    m = me % KVH
    is_root = me == 0
    is_last = p == planes - 1
    low = m // 2 * 2
    far = (m + 2) % KVH

    def cols(g):
        return pl.ds(pl.multiple_of(g * DH, DH), DH)

    def wide(g):
        return pl.ds(pl.multiple_of(g * (G * DH), G * DH), G * DH)

    def load_kv(g, i, half, sem):
        src = (ctx_k, ctx_v)[i]
        return pltpu.make_async_copy(src.at[:, cols(g)], kc.at[g, i, half], sem.at[g, i])

    for g in range(KVH):
        for i in range(2):
            load_kv(g, i, 1, s_kv).start()

    @pl.when(is_root)
    def _():
        for g in range(KVH):
            for i in range(2):
                load_kv(g, i, 0, s_an).start()

    own_copies = [
        pltpu.make_async_copy(pack.at[m, 0], qall.at[me], s_own.at[0]),
        pltpu.make_async_copy(pack.at[0, 3], cnt.at[m], s_own.at[1]),
        pltpu.make_async_copy(ctx_k.at[:, cols(m)], kvall.at[m, 0], s_own.at[2]),
        pltpu.make_async_copy(ctx_v.at[:, cols(m)], kvall.at[m, 1], s_own.at[3]),
    ]
    own_self = pltpu.make_async_copy(pack.at[m, pl.ds(1, 2)], selfkv.at[me], s_own.at[4])
    q_loads = [
        pltpu.make_async_copy(ctx_q.at[:, wide(g)], qbuf.at[:, wide(g)], s_q.at[g])
        for g in range(KVH)
    ]
    for copy in own_copies:
        copy.start()

    @pl.when(is_last)
    def _():
        own_self.start()

    for copy in q_loads:
        copy.start()

    barrier = pltpu.get_barrier_semaphore()

    @pl.loop(1, n)
    def _(d):
        pl.semaphore_signal(
            barrier, inc=1, device_id={"hst": (me + d) % n}, device_id_type=pl.DeviceIdType.MESH
        )

    pl.semaphore_wait(barrier, n - 1)

    def q_send(d):
        target = (me + d) % n
        return remote(pack.at[target % KVH, 0], qall.at[me], q_s.at[d], q_r.at[me], target)

    @pl.loop(1, n)
    def _(d):
        q_send(d).start()

    def self_send(g):
        return remote(
            pack.at[g, pl.ds(1, 2)], selfkv.at[me], f_s.at[g], r_s.at[me], n - KVH + g
        )

    for g in range(KVH):
        @pl.when(me != n - KVH + g)
        def _():
            self_send(g).start()

    def cnt_send(d):
        g = (m + d) % KVH
        return remote(pack.at[0, 3], cnt.at[m], c_s.at[d], c_r.at[m], p * KVH + g)

    for d in range(1, KVH):
        cnt_send(d).start()

    for g in range(KVH):
        for i in range(2):
            load_kv(g, i, 1, s_kv).wait()

    def chunk_send(g, slot, target):
        piece = kc.at[g, :, 0]
        return remote(piece, piece, a_s.at[g, slot], a_r.at[g], target)

    def across(g):
        return chunk_send(g, 0, p * KVH + far)

    def beside(g):
        return chunk_send(g, 1, p * KVH + m + 1)

    def along(g, q):
        return chunk_send(g, 1 + q, q * KVH + m)

    even = m % 2 == 0
    first = [low, low + 1]
    second = [far // 2 * 2, far // 2 * 2 + 1]

    @pl.when(is_root)
    def _():
        for g in range(KVH):
            for i in range(2):
                load_kv(g, i, 0, s_an).wait()
        for g in (2, 3):
            across(g).start()
        for q in range(planes - 1, 0, -1):
            for g in (0, 1):
                along(g, q).start()

    def kv_send(d):
        g = (m + d) % KVH
        return remote(kc.at[g, :, 1], kvall.at[m], k_s.at[d], k_r.at[m], p * KVH + g)

    for d in (2, 3, 1):
        kv_send(d).start()

    @pl.when(is_root)
    def _():
        for g in (0, 1):
            across(g).start()
        for g in (0, 1, 2, 3):
            beside(g).start()

    def chunk_wait(g):
        chunk_send(g, 0, me).wait_recv()

    hub = (p == 0) & (m == 2)

    def take_first():
        @pl.when(jnp.logical_not(is_root))
        def _():
            for g in first:
                chunk_wait(g)

                @pl.when(hub)
                def _():
                    for q in range(planes - 1, 0, -1):
                        along(g, q).start()

                @pl.when(even & (p > 0))
                def _():
                    across(g).start()

                @pl.when(even)
                def _():
                    beside(g).start()

    def take_second():
        @pl.when(jnp.logical_not(is_root))
        def _():
            for g in second:
                chunk_wait(g)

                @pl.when(even)
                def _():
                    beside(g).start()

    early = hub | ((m == 0) & (p > 0))

    @pl.when(early)
    def _():
        take_first()

    @pl.loop(1, n)
    def _(d):
        source = (me + d) % n
        remote(pack.at[0, 0], qall.at[source], q_s.at[0], q_r.at[source], me).wait_recv()

    for copy in own_copies:
        copy.wait()

    for d in range(1, KVH):
        j = (m + d) % KVH
        remote(pack.at[0, 3], cnt.at[j], c_s.at[0], c_r.at[j], me).wait_recv()
        remote(kc.at[0, :, 1], kvall.at[j], k_s.at[0], k_r.at[j], me).wait_recv()

    def diagonal():
        return lax.broadcasted_iota(jnp.int32, (span, DH), 0) == lax.broadcasted_iota(
            jnp.int32, (span, DH), 1
        )

    def num_send(q):
        return remote(num.at[q], numr.at[p], n_s.at[q], n_r.at[p], q * KVH + m)

    def ask(with_self):
        total_rows = PAIR * span
        lane = lax.broadcasted_iota(jnp.int32, (total_rows, rows), 1).astype(jnp.float32)

        @pl.loop(0, planes // PAIR)
        def _(step):
            at_planes = [(p + 1 + step * PAIR + k) % planes for k in range(PAIR)]
            queries = jnp.concatenate(
                [qall[pl.ds(q * KVH, KVH)].reshape(span, DH) for q in at_planes], axis=0
            )
            s = [
                lax.dot_general(queries, kvall[j, 0], NT, preferred_element_type=jnp.float32)
                for j in range(KVH)
            ]
            s = [
                jnp.where(lane < cnt[j].astype(jnp.float32)[0:1, :], s[j], -jnp.inf)
                for j in range(KVH)
            ]
            values = [kvall[j, 1] for j in range(KVH)]
            top = [jnp.max(x, axis=1, keepdims=True) for x in s]
            if with_self:
                keys = selfkv[:, 0].reshape(n * tile, DH)
                s2 = lax.dot_general(queries, keys, NT, preferred_element_type=jnp.float32)
                shape = (total_rows, n * tile)
                at = lax.broadcasted_iota(jnp.int32, shape, 1)
                row = lax.broadcasted_iota(jnp.int32, shape, 0)
                base = jnp.where(row < span, at_planes[0] * span, at_planes[-1] * span - span)
                shift = tile.bit_length() - 1
                u = (at >> shift) * tokens + (at & (tile - 1))
                t = (base + row) >> (G.bit_length() - 1)
                s2 = jnp.where(((at & (tile - 1)) < tokens) & (u <= t), s2, -jnp.inf)
                s[-1] = jnp.concatenate([s[-1], s2], axis=1)
                values[-1] = jnp.concatenate(
                    [values[-1], selfkv[:, 1].reshape(n * tile, DH)], axis=0
                )
                top[-1] = jnp.maximum(top[-1], jnp.max(s2, axis=1, keepdims=True))
            e = [jnp.exp2((x - y) * C) for x, y in zip(s, top)]
            part = [jnp.sum(x, axis=1, keepdims=True) for x in e]
            mixed = [
                lax.dot_general(
                    x.astype(jnp.bfloat16), v, NN, preferred_element_type=jnp.float32
                )
                for x, v in zip(e, values)
            ]
            best = functools.reduce(jnp.maximum, top)
            factor = [jnp.exp2((x - best) * C) for x in top]
            total = sum(x * y for x, y in zip(part, factor))
            summed = sum(x * y for x, y in zip(mixed, factor))
            diag = diagonal()
            pick = lax.broadcasted_iota(jnp.int32, (8, DH), 0) == 0
            for k, q in enumerate(at_planes):
                cut = slice(k * span, (k + 1) * span)
                num[q, pl.ds(0, span)] = summed[cut]
                line1 = jnp.sum(jnp.where(diag, best[cut], 0.0), axis=0, keepdims=True)
                line2 = jnp.sum(jnp.where(diag, total[cut], 0.0), axis=0, keepdims=True)
                num[q, pl.ds(span, 8)] = jnp.where(pick, line1, line2)
            for q in at_planes:
                @pl.when(q != p)
                def _():
                    num_send(q).start()

    @pl.when(is_last)
    def _():
        own_self.wait()

        @pl.loop(1, n)
        def _(d):
            source = (me + d) % n
            remote(
                pack.at[0, pl.ds(1, 2)], selfkv.at[source], f_s.at[0], r_s.at[source], me
            ).wait_recv()

        ask(True)

    @pl.when(jnp.logical_not(is_last))
    def _():
        ask(False)

    def out_copy(g):
        return pltpu.make_async_copy(obuf.at[:, wide(g)], ctx_out.at[:, wide(g)], s_out.at[g])

    def context(g):
        pltpu.make_async_copy(ctx_q.at[:, wide(g)], qbuf.at[:, wide(g)], s_q.at[g]).wait()
        count = cnt[m].astype(jnp.float32)[0:1, :]
        row = lax.broadcasted_iota(jnp.int32, (rows, rows), 0)
        lane = lax.broadcasted_iota(jnp.int32, (rows, rows), 1)
        own = (lane <= row) & (lane.astype(jnp.float32) < count)
        outer = jnp.broadcast_to(me, (rows, rows)) > 0
        visible = jnp.concatenate([outer, own], axis=1)
        kept = lax.broadcasted_iota(jnp.int32, (rows, DH), 0).astype(jnp.float32) < count

        @pl.loop(0, G // UNROLL)
        def _(step):
            keys = kc[g, 0].reshape(2 * rows, DH)
            values = kc[g, 1].reshape(2 * rows, DH)
            at = [
                pl.ds(pl.multiple_of((g * G + step * UNROLL + k) * DH, DH), DH)
                for k in range(UNROLL)
            ]
            s = [
                lax.dot_general(qbuf[:, x], keys, NT, preferred_element_type=jnp.float32)
                for x in at
            ]
            s = [jnp.where(visible, x, -jnp.inf) for x in s]
            top = [jnp.max(x, axis=1, keepdims=True) for x in s]
            e = [jnp.exp2((x - y) * C) for x, y in zip(s, top)]
            total = [jnp.sum(x, axis=1, keepdims=True) for x in e]
            mixed = [
                lax.dot_general(
                    x.astype(jnp.bfloat16), values, NN, preferred_element_type=jnp.float32
                )
                for x in e
            ]
            for k in range(UNROLL):
                out = jnp.where(kept, mixed[k] * (1.0 / total[k]), 0.0)
                obuf[:, at[k]] = out.astype(jnp.bfloat16)

        out_copy(g).start()

    @pl.when(jnp.logical_not(early))
    def _():
        take_first()

    context(first[0])
    take_second()
    context(first[1])
    context(second[0])

    @pl.loop(1, planes)
    def _(d):
        q = (p + d) % planes
        remote(num.at[0], numr.at[q], n_s.at[0], n_r.at[q], me).wait_recv()

    def columns(block):
        diag = diagonal()
        best = jnp.sum(jnp.where(diag, block[0:1, :], 0.0), axis=1, keepdims=True)
        total = jnp.sum(jnp.where(diag, block[1:2, :], 0.0), axis=1, keepdims=True)
        return best, total

    best, total = columns(num[p, pl.ds(span, 8)])
    summed = num[p, pl.ds(0, span)]
    for d in range(1, planes):
        q = (p + d) % planes
        top, part = columns(numr[q, pl.ds(span, 8)])
        mixed = numr[q, pl.ds(0, span)]
        peak = jnp.maximum(best, top)
        old = jnp.exp2((best - peak) * C)
        new = jnp.exp2((top - peak) * C)
        best, total, summed = peak, total * old + part * new, summed * old + mixed * new
    fin[...] = (summed * (1.0 / total)).astype(jnp.bfloat16).reshape(KVH, tile, DH)

    def fin_send(d):
        j = (m + d) % KVH
        return remote(fin.at[j], ask_out.at[m], o_s.at[d], o_r.at[m], p * KVH + j)

    own_fin = pltpu.make_async_copy(fin.at[m], ask_out.at[m], s_own.at[5])
    for d in range(1, KVH):
        fin_send(d).start()
    own_fin.start()

    context(second[1])

    own_fin.wait()
    for d in range(1, KVH):
        j = (m + d) % KVH
        remote(fin.at[0], ask_out.at[j], o_s.at[0], o_r.at[j], me).wait_recv()
        fin_send(d).wait_send()
        cnt_send(d).wait_send()
        kv_send(d).wait_send()
    for g in range(KVH):
        out_copy(g).wait()

        @pl.when(me != n - KVH + g)
        def _():
            self_send(g).wait_send()

    @pl.loop(1, n)
    def _(d):
        q_send(d).wait_send()

    @pl.loop(1, planes)
    def _(d):
        num_send((p + d) % planes).wait_send()

    @pl.when(is_root)
    def _():
        for g in range(KVH):
            across(g).wait_send()
            beside(g).wait_send()
        for q in range(1, planes):
            for g in (0, 1):
                along(g, q).wait_send()

    @pl.when(even & jnp.logical_not(is_root))
    def _():
        for g in first + second:
            beside(g).wait_send()

        @pl.when(p > 0)
        def _():
            for g in first:
                across(g).wait_send()

    @pl.when(hub)
    def _():
        for g in first:
            for q in range(1, planes):
                along(g, q).wait_send()


def body(n, ctx_q, ctx_k, ctx_v, ask_q, ask_k, ask_v, valid):
    rows = ctx_q.shape[0]
    tokens = ask_q.shape[0]
    tile = tokens * G
    planes = n // KVH
    span = KVH * tile

    def heads(x):
        x = x.reshape(tokens, KVH, -1, DH).transpose(1, 0, 2, 3).reshape(KVH, -1, DH)
        return jnp.pad(x, ((0, 0), (0, tile - x.shape[1]), (0, 0)))

    count = jnp.broadcast_to(valid.astype(jnp.bfloat16).reshape(1, 1, 1), (KVH, tile, DH))
    pack = jnp.stack([heads(ask_q), heads(ask_k), heads(ask_v), count], axis=1)
    dma = pltpu.SemaphoreType.DMA
    bf = jnp.bfloat16
    ctx_out, ask_out = pl.pallas_call(
        functools.partial(kernel, n),
        out_shape=(
            jax.ShapeDtypeStruct(ctx_q.shape, bf),
            jax.ShapeDtypeStruct((KVH, tile, DH), bf),
        ),
        in_specs=[pl.BlockSpec(memory_space=pl.ANY)] * 4,
        out_specs=(pl.BlockSpec(memory_space=pl.ANY),) * 2,
        scratch_shapes=[
            pltpu.VMEM(ctx_q.shape, bf),
            pltpu.VMEM(ctx_q.shape, bf),
            pltpu.VMEM((KVH, 2, 2, rows, DH), bf),
            pltpu.VMEM((KVH, 2, rows, DH), bf),
            pltpu.VMEM((KVH, tile, DH), bf),
            pltpu.VMEM((n, tile, DH), bf),
            pltpu.VMEM((n, 2, tile, DH), bf),
            pltpu.VMEM((planes, span + 8, DH), jnp.float32),
            pltpu.VMEM((planes, span + 8, DH), jnp.float32),
            pltpu.VMEM((KVH, tile, DH), bf),
            dma((KVH, 2)),
            dma((KVH, 2)),
            dma((KVH,)),
            dma((KVH,)),
            dma((6,)),
            dma((n,)),
            dma((n,)),
            dma((KVH,)),
            dma((KVH,)),
            dma((KVH,)),
            dma((KVH,)),
            dma((KVH, planes + 1)),
            dma((KVH,)),
            dma((KVH,)),
            dma((n,)),
            dma((planes,)),
            dma((planes,)),
            dma((KVH,)),
            dma((KVH,)),
        ],
        compiler_params=pltpu.CompilerParams(collective_id=0, has_side_effects=True),
    )(ctx_q, ctx_k, ctx_v, pack)
    ask_out = ask_out.reshape(KVH, tokens, G, DH).transpose(1, 0, 2, 3).reshape(tokens, H * DH)
    return ctx_out, ask_out


def solution(mesh):
    n = mesh.shape["hst"]
    rows = P(("req", "hst"), None)
    return jax.shard_map(
        functools.partial(body, n),
        mesh=mesh,
        in_specs=(rows,) * 6 + (P(("req", "hst")),),
        out_specs=(rows, rows),
        check_vma=False,
    )
```

```python
import functools
import math

import jax
import jax.numpy as jnp
from jax import lax
from jax.experimental import pallas as pl
from jax.experimental.pallas import tpu as pltpu
from jax.sharding import PartitionSpec as P

H = 32
KVH = 4
DH = 128
G = H // KVH
UNROLL = 8
PAIR = 2
C = math.log2(math.e) / math.sqrt(DH)
NT = (((1,), (1,)), ((), ()))
NN = (((1,), (0,)), ((), ()))


def remote(src, dst, send_sem, recv_sem, target):
    return pltpu.make_async_remote_copy(
        src_ref=src,
        dst_ref=dst,
        send_sem=send_sem,
        recv_sem=recv_sem,
        device_id={"hst": target},
        device_id_type=pl.DeviceIdType.MESH,
    )


def kernel(
    n, ctx_q, ctx_k, ctx_v, pack, ctx_out, ask_out,
    qbuf, obuf, kc, kvall, cnt, qall, selfkv, num, numr, fin,
    s_kv, s_an, s_q, s_out, s_own,
    q_s, q_r, k_s, k_r, c_s, c_r, a_s, a_r, f_s, r_s, n_s, n_r, o_s, o_r,
):
    rows = ctx_q.shape[0]
    tile = pack.shape[2]
    tokens = tile // G
    planes = n // KVH
    span = KVH * tile
    me = lax.axis_index("hst")
    p = me // KVH
    m = me % KVH
    is_root = me == 0
    is_last = p == planes - 1
    low = m // 2 * 2
    far = (m + 2) % KVH

    def cols(g):
        return pl.ds(pl.multiple_of(g * DH, DH), DH)

    def wide(g):
        return pl.ds(pl.multiple_of(g * (G * DH), G * DH), G * DH)

    def load_kv(g, i, half, sem):
        src = (ctx_k, ctx_v)[i]
        return pltpu.make_async_copy(src.at[:, cols(g)], kc.at[g, i, half], sem.at[g, i])

    for g in range(KVH):
        for i in range(2):
            load_kv(g, i, 1, s_kv).start()

    @pl.when(is_root)
    def _():
        for g in range(KVH):
            for i in range(2):
                load_kv(g, i, 0, s_an).start()

    own_copies = [
        pltpu.make_async_copy(pack.at[m, 0], qall.at[me], s_own.at[0]),
        pltpu.make_async_copy(pack.at[0, 3], cnt.at[m], s_own.at[1]),
        pltpu.make_async_copy(ctx_k.at[:, cols(m)], kvall.at[m, 0], s_own.at[2]),
        pltpu.make_async_copy(ctx_v.at[:, cols(m)], kvall.at[m, 1], s_own.at[3]),
    ]
    own_self = pltpu.make_async_copy(pack.at[m, pl.ds(1, 2)], selfkv.at[me], s_own.at[4])
    q_loads = [
        pltpu.make_async_copy(ctx_q.at[:, wide(g)], qbuf.at[:, wide(g)], s_q.at[g])
        for g in range(KVH)
    ]
    for copy in own_copies:
        copy.start()

    @pl.when(is_last)
    def _():
        own_self.start()

    for copy in q_loads:
        copy.start()

    barrier = pltpu.get_barrier_semaphore()

    @pl.loop(1, n)
    def _(d):
        pl.semaphore_signal(
            barrier, inc=1, device_id={"hst": (me + d) % n}, device_id_type=pl.DeviceIdType.MESH
        )

    pl.semaphore_wait(barrier, n - 1)

    def q_send(d):
        target = (me + d) % n
        return remote(pack.at[target % KVH, 0], qall.at[me], q_s.at[d], q_r.at[me], target)

    @pl.loop(1, n)
    def _(d):
        q_send(d).start()

    def self_send(g):
        return remote(
            pack.at[g, pl.ds(1, 2)], selfkv.at[me], f_s.at[g], r_s.at[me], n - KVH + g
        )

    for g in range(KVH):
        @pl.when(me != n - KVH + g)
        def _():
            self_send(g).start()

    def cnt_send(d):
        g = (m + d) % KVH
        return remote(pack.at[0, 3], cnt.at[m], c_s.at[d], c_r.at[m], p * KVH + g)

    for d in range(1, KVH):
        cnt_send(d).start()

    for g in range(KVH):
        for i in range(2):
            load_kv(g, i, 1, s_kv).wait()

    def chunk_send(g, slot, target):
        piece = kc.at[g, :, 0]
        return remote(piece, piece, a_s.at[g, slot], a_r.at[g], target)

    def across(g):
        return chunk_send(g, 0, p * KVH + far)

    def beside(g):
        return chunk_send(g, 1, p * KVH + m + 1)

    def along(g, q):
        return chunk_send(g, 1 + q, q * KVH + m)

    even = m % 2 == 0
    first = [low, low + 1]
    second = [far // 2 * 2, far // 2 * 2 + 1]

    @pl.when(is_root)
    def _():
        for g in range(KVH):
            for i in range(2):
                load_kv(g, i, 0, s_an).wait()
        for g in (2, 3):
            across(g).start()
        for q in range(planes - 1, 0, -1):
            for g in (0, 1):
                along(g, q).start()

    def kv_send(d):
        g = (m + d) % KVH
        return remote(kc.at[g, :, 1], kvall.at[m], k_s.at[d], k_r.at[m], p * KVH + g)

    for d in (2, 3, 1):
        kv_send(d).start()

    @pl.when(is_root)
    def _():
        for g in (0, 1):
            across(g).start()
        for g in (0, 1, 2, 3):
            beside(g).start()

    def chunk_wait(g):
        chunk_send(g, 0, me).wait_recv()

    hub = (p == 0) & (m == 2)

    def take_first():
        @pl.when(jnp.logical_not(is_root))
        def _():
            for g in first:
                chunk_wait(g)

                @pl.when(hub)
                def _():
                    for q in range(planes - 1, 0, -1):
                        along(g, q).start()

                @pl.when(even & (p > 0))
                def _():
                    across(g).start()

                @pl.when(even)
                def _():
                    beside(g).start()

    def take_second():
        @pl.when(jnp.logical_not(is_root))
        def _():
            for g in second:
                chunk_wait(g)

                @pl.when(even)
                def _():
                    beside(g).start()

    early = hub | ((m == 0) & (p > 0))

    @pl.when(early)
    def _():
        take_first()

    @pl.loop(1, n)
    def _(d):
        source = (me + d) % n
        remote(pack.at[0, 0], qall.at[source], q_s.at[0], q_r.at[source], me).wait_recv()

    for copy in own_copies:
        copy.wait()

    for d in range(1, KVH):
        j = (m + d) % KVH
        remote(pack.at[0, 3], cnt.at[j], c_s.at[0], c_r.at[j], me).wait_recv()
        remote(kc.at[0, :, 1], kvall.at[j], k_s.at[0], k_r.at[j], me).wait_recv()

    def diagonal():
        return lax.broadcasted_iota(jnp.int32, (span, DH), 0) == lax.broadcasted_iota(
            jnp.int32, (span, DH), 1
        )

    def num_send(q):
        return remote(num.at[q], numr.at[p], n_s.at[q], n_r.at[p], q * KVH + m)

    def ask(with_self):
        total_rows = PAIR * span
        lane = lax.broadcasted_iota(jnp.int32, (total_rows, rows), 1).astype(jnp.float32)

        @pl.loop(0, planes // PAIR)
        def _(step):
            at_planes = [(p + 1 + step * PAIR + k) % planes for k in range(PAIR)]
            queries = jnp.concatenate(
                [qall[pl.ds(q * KVH, KVH)].reshape(span, DH) for q in at_planes], axis=0
            )
            s = [
                lax.dot_general(queries, kvall[j, 0], NT, preferred_element_type=jnp.float32)
                for j in range(KVH)
            ]
            s = [
                jnp.where(lane < cnt[j].astype(jnp.float32)[0:1, :], s[j], -jnp.inf)
                for j in range(KVH)
            ]
            values = [kvall[j, 1] for j in range(KVH)]
            top = [jnp.max(x, axis=1, keepdims=True) for x in s]
            if with_self:
                keys = selfkv[:, 0].reshape(n * tile, DH)
                s2 = lax.dot_general(queries, keys, NT, preferred_element_type=jnp.float32)
                shape = (total_rows, n * tile)
                at = lax.broadcasted_iota(jnp.int32, shape, 1)
                row = lax.broadcasted_iota(jnp.int32, shape, 0)
                base = jnp.where(row < span, at_planes[0] * span, at_planes[-1] * span - span)
                shift = tile.bit_length() - 1
                u = (at >> shift) * tokens + (at & (tile - 1))
                t = (base + row) >> (G.bit_length() - 1)
                s2 = jnp.where(((at & (tile - 1)) < tokens) & (u <= t), s2, -jnp.inf)
                s[-1] = jnp.concatenate([s[-1], s2], axis=1)
                values[-1] = jnp.concatenate(
                    [values[-1], selfkv[:, 1].reshape(n * tile, DH)], axis=0
                )
                top[-1] = jnp.maximum(top[-1], jnp.max(s2, axis=1, keepdims=True))
            e = [jnp.exp2((x - y) * C) for x, y in zip(s, top)]
            part = [jnp.sum(x, axis=1, keepdims=True) for x in e]
            mixed = [
                lax.dot_general(
                    x.astype(jnp.bfloat16), v, NN, preferred_element_type=jnp.float32
                )
                for x, v in zip(e, values)
            ]
            best = functools.reduce(jnp.maximum, top)
            factor = [jnp.exp2((x - best) * C) for x in top]
            total = sum(x * y for x, y in zip(part, factor))
            summed = sum(x * y for x, y in zip(mixed, factor))
            diag = diagonal()
            pick = lax.broadcasted_iota(jnp.int32, (8, DH), 0) == 0
            for k, q in enumerate(at_planes):
                cut = slice(k * span, (k + 1) * span)
                num[q, pl.ds(0, span)] = summed[cut]
                line1 = jnp.sum(jnp.where(diag, best[cut], 0.0), axis=0, keepdims=True)
                line2 = jnp.sum(jnp.where(diag, total[cut], 0.0), axis=0, keepdims=True)
                num[q, pl.ds(span, 8)] = jnp.where(pick, line1, line2)
            for q in at_planes:
                @pl.when(q != p)
                def _():
                    num_send(q).start()

    @pl.when(is_last)
    def _():
        own_self.wait()

        @pl.loop(1, n)
        def _(d):
            source = (me + d) % n
            remote(
                pack.at[0, pl.ds(1, 2)], selfkv.at[source], f_s.at[0], r_s.at[source], me
            ).wait_recv()

        ask(True)

    @pl.when(jnp.logical_not(is_last))
    def _():
        ask(False)

    def out_copy(g):
        return pltpu.make_async_copy(obuf.at[:, wide(g)], ctx_out.at[:, wide(g)], s_out.at[g])

    def context(g):
        pltpu.make_async_copy(ctx_q.at[:, wide(g)], qbuf.at[:, wide(g)], s_q.at[g]).wait()
        count = cnt[m].astype(jnp.float32)[0:1, :]
        row = lax.broadcasted_iota(jnp.int32, (rows, rows), 0)
        lane = lax.broadcasted_iota(jnp.int32, (rows, rows), 1)
        own = (lane <= row) & (lane.astype(jnp.float32) < count)
        outer = jnp.broadcast_to(me, (rows, rows)) > 0
        visible = jnp.concatenate([outer, own], axis=1)
        kept = lax.broadcasted_iota(jnp.int32, (rows, DH), 0).astype(jnp.float32) < count

        @pl.loop(0, G // UNROLL)
        def _(step):
            keys = kc[g, 0].reshape(2 * rows, DH)
            values = kc[g, 1].reshape(2 * rows, DH)
            at = [
                pl.ds(pl.multiple_of((g * G + step * UNROLL + k) * DH, DH), DH)
                for k in range(UNROLL)
            ]
            s = [
                lax.dot_general(qbuf[:, x], keys, NT, preferred_element_type=jnp.float32)
                for x in at
            ]
            s = [jnp.where(visible, x, -jnp.inf) for x in s]
            top = [jnp.max(x, axis=1, keepdims=True) for x in s]
            e = [jnp.exp2((x - y) * C) for x, y in zip(s, top)]
            total = [jnp.sum(x, axis=1, keepdims=True) for x in e]
            mixed = [
                lax.dot_general(
                    x.astype(jnp.bfloat16), values, NN, preferred_element_type=jnp.float32
                )
                for x in e
            ]
            for k in range(UNROLL):
                out = jnp.where(kept, mixed[k] * (1.0 / total[k]), 0.0)
                obuf[:, at[k]] = out.astype(jnp.bfloat16)

        out_copy(g).start()

    @pl.when(jnp.logical_not(early))
    def _():
        take_first()

    context(first[0])
    take_second()
    context(first[1])

    @pl.loop(1, planes)
    def _(d):
        q = (p + d) % planes
        remote(num.at[0], numr.at[q], n_s.at[0], n_r.at[q], me).wait_recv()

    def columns(block):
        diag = diagonal()
        best = jnp.sum(jnp.where(diag, block[0:1, :], 0.0), axis=1, keepdims=True)
        total = jnp.sum(jnp.where(diag, block[1:2, :], 0.0), axis=1, keepdims=True)
        return best, total

    best, total = columns(num[p, pl.ds(span, 8)])
    summed = num[p, pl.ds(0, span)]
    for d in range(1, planes):
        q = (p + d) % planes
        top, part = columns(numr[q, pl.ds(span, 8)])
        mixed = numr[q, pl.ds(0, span)]
        peak = jnp.maximum(best, top)
        old = jnp.exp2((best - peak) * C)
        new = jnp.exp2((top - peak) * C)
        best, total, summed = peak, total * old + part * new, summed * old + mixed * new
    fin[...] = (summed * (1.0 / total)).astype(jnp.bfloat16).reshape(KVH, tile, DH)

    def fin_send(d):
        j = (m + d) % KVH
        return remote(fin.at[j], ask_out.at[m], o_s.at[d], o_r.at[m], p * KVH + j)

    own_fin = pltpu.make_async_copy(fin.at[m], ask_out.at[m], s_own.at[5])
    for d in range(1, KVH):
        fin_send(d).start()
    own_fin.start()

    context(second[0])
    context(second[1])

    own_fin.wait()
    for d in range(1, KVH):
        j = (m + d) % KVH
        remote(fin.at[0], ask_out.at[j], o_s.at[0], o_r.at[j], me).wait_recv()
        fin_send(d).wait_send()
        cnt_send(d).wait_send()
        kv_send(d).wait_send()
    for g in range(KVH):
        out_copy(g).wait()

        @pl.when(me != n - KVH + g)
        def _():
            self_send(g).wait_send()

    @pl.loop(1, n)
    def _(d):
        q_send(d).wait_send()

    @pl.loop(1, planes)
    def _(d):
        num_send((p + d) % planes).wait_send()

    @pl.when(is_root)
    def _():
        for g in range(KVH):
            across(g).wait_send()
            beside(g).wait_send()
        for q in range(1, planes):
            for g in (0, 1):
                along(g, q).wait_send()

    @pl.when(even & jnp.logical_not(is_root))
    def _():
        for g in first + second:
            beside(g).wait_send()

        @pl.when(p > 0)
        def _():
            for g in first:
                across(g).wait_send()

    @pl.when(hub)
    def _():
        for g in first:
            for q in range(1, planes):
                along(g, q).wait_send()


def body(n, ctx_q, ctx_k, ctx_v, ask_q, ask_k, ask_v, valid):
    rows = ctx_q.shape[0]
    tokens = ask_q.shape[0]
    tile = tokens * G
    planes = n // KVH
    span = KVH * tile

    def heads(x):
        x = x.reshape(tokens, KVH, -1, DH).transpose(1, 0, 2, 3).reshape(KVH, -1, DH)
        return jnp.pad(x, ((0, 0), (0, tile - x.shape[1]), (0, 0)))

    count = jnp.broadcast_to(valid.astype(jnp.bfloat16).reshape(1, 1, 1), (KVH, tile, DH))
    pack = jnp.stack([heads(ask_q), heads(ask_k), heads(ask_v), count], axis=1)
    dma = pltpu.SemaphoreType.DMA
    bf = jnp.bfloat16
    ctx_out, ask_out = pl.pallas_call(
        functools.partial(kernel, n),
        out_shape=(
            jax.ShapeDtypeStruct(ctx_q.shape, bf),
            jax.ShapeDtypeStruct((KVH, tile, DH), bf),
        ),
        in_specs=[pl.BlockSpec(memory_space=pl.ANY)] * 4,
        out_specs=(pl.BlockSpec(memory_space=pl.ANY),) * 2,
        scratch_shapes=[
            pltpu.VMEM(ctx_q.shape, bf),
            pltpu.VMEM(ctx_q.shape, bf),
            pltpu.VMEM((KVH, 2, 2, rows, DH), bf),
            pltpu.VMEM((KVH, 2, rows, DH), bf),
            pltpu.VMEM((KVH, tile, DH), bf),
            pltpu.VMEM((n, tile, DH), bf),
            pltpu.VMEM((n, 2, tile, DH), bf),
            pltpu.VMEM((planes, span + 8, DH), jnp.float32),
            pltpu.VMEM((planes, span + 8, DH), jnp.float32),
            pltpu.VMEM((KVH, tile, DH), bf),
            dma((KVH, 2)),
            dma((KVH, 2)),
            dma((KVH,)),
            dma((KVH,)),
            dma((6,)),
            dma((n,)),
            dma((n,)),
            dma((KVH,)),
            dma((KVH,)),
            dma((KVH,)),
            dma((KVH,)),
            dma((KVH, planes + 1)),
            dma((KVH,)),
            dma((KVH,)),
            dma((n,)),
            dma((planes,)),
            dma((planes,)),
            dma((KVH,)),
            dma((KVH,)),
        ],
        compiler_params=pltpu.CompilerParams(collective_id=0, has_side_effects=True),
    )(ctx_q, ctx_k, ctx_v, pack)
    ask_out = ask_out.reshape(KVH, tokens, G, DH).transpose(1, 0, 2, 3).reshape(tokens, H * DH)
    return ctx_out, ask_out


def solution(mesh):
    n = mesh.shape["hst"]
    rows = P(("req", "hst"), None)
    return jax.shard_map(
        functools.partial(body, n),
        mesh=mesh,
        in_specs=(rows,) * 6 + (P(("req", "hst")),),
        out_specs=(rows, rows),
        check_vma=False,
    )
```
